256 devices in a mesh: seg: 8 (over y, core), op: 32 (over z, x).
Axes of the slice: x: 4, y: 4, z: 8, core: 2. Of those that a mesh axis runs over, the one named last changes fastest.
Arguments:
- psi_start: bfloat16 [8, 32, 128, 128], P('seg', 'op'), may hold values from -4 to 4
- left_ops: bfloat16 [8, 128, 32, 128, 128], P('seg', 'op'), may hold values from -2 to 9, as said below
- right_ops: bfloat16 [8, 128, 32, 128, 128], P('seg', 'op'), may hold values from -2 to 9, as said below
- shifts: int32 [8, 128], P('seg', 'op'), may hold values from 0 to 31
- active: int32 [8, 128, 32], P('seg', 'op'), may hold values 0 or 1
Outputs:
- state: bfloat16 [8, 32, 128, 128], P('seg', 'op')
- rdm_pieces: float32 [8, 128], P('seg', 'op')
The draws below stay inside these ranges and needn't reach their ends.
Inputs may be any that keep to these rules, and one draw needn't show every extreme that they name: `left_ops`: each block is a diagonal of entries between 1 and 7.8 plus off-diagonal entries of size about 2 / sqrt(128). `right_ops`: each block is a diagonal of entries between 1 and 7.8 plus off-diagonal entries of size about 2 / sqrt(128).
All inputs are finite; a program needn't handle non-finite values. No bound on the sum of `active` on one device may be relied on, other than what follows from the above.
Results may differ from the reference program's by a relative error of at most 0.0046.
Values may be sent and summed in bfloat16 or wider, within the bound.
A program may use at most 64 MiB of HBM per device.

```python
import jax
import jax.numpy as jnp
from jax import lax

QB = 128
SECT = 32
ITERS = 3
TERMS = 128
SEGS = 8
N_SEG = 8


def dominant_blocks(key, shape, diag_low, diag_high, noise_scale, flat_noise):
    key_diag, key_noise = jax.random.split(key)
    width = shape[-1]
    diagonal = jax.random.uniform(key_diag, shape[:-1], jnp.float32, diag_low, diag_high)
    if flat_noise:
        noise = jax.random.uniform(key_noise, shape, jnp.float32, -1.7, 1.7)
    else:
        noise = jnp.clip(jax.random.normal(key_noise, shape, jnp.float32), -4.0, 4.0)
    rows = lax.broadcasted_iota(jnp.int32, (width, width), 0)
    cols = lax.broadcasted_iota(jnp.int32, (width, width), 1)
    identity = (rows == cols).astype(jnp.float32)
    return noise * (noise_scale / jnp.sqrt(float(width))) + identity * diagonal[..., None]


def draw_psi_start(key, part):
    shape = (SEGS, SECT, QB, QB)
    values = jnp.clip(jax.random.normal(jax.random.fold_in(key, 5), shape, jnp.float32), -4.0, 4.0)
    return values.astype(jnp.bfloat16)


def draw_left_ops(key, part):
    shape = (SEGS, TERMS, SECT, QB, QB)
    blocks = dominant_blocks(jax.random.fold_in(key, 11), shape, 2.0, 6.0, 2.0, False)
    return blocks.astype(jnp.bfloat16)


def draw_right_ops(key, part):
    shape = (SEGS, TERMS, SECT, QB, QB)
    blocks = dominant_blocks(jax.random.fold_in(key, 23), shape, 2.0, 6.0, 2.0, False)
    return blocks.astype(jnp.bfloat16)


def place_ends(values, stream_key, low, largest):
    longest = values.shape.index(max(values.shape))
    spots = []
    for shift in (0, 1):
        where = [jax.random.randint(jax.random.fold_in(stream_key, axis), (), 0, length) for axis, length in enumerate(values.shape)]
        where[longest] = (where[longest] + shift) % values.shape[longest]
        spots.append(tuple(where))
    return values.at[spots[0]].set(low).at[spots[1]].set(largest)


def setup_inputs(seed: int = 0) -> dict:
    splits = jax.random.split(jax.random.key(seed), 6)
    return {
        "psi_start": draw_psi_start(jax.random.fold_in(splits[5], 71), 0),
        "left_ops": draw_left_ops(jax.random.fold_in(splits[5], 71), 0),
        "right_ops": draw_right_ops(jax.random.fold_in(splits[5], 71), 0),
        "shifts": place_ends(jax.random.randint(splits[3], (SEGS, TERMS), 0, SECT), jax.random.fold_in(splits[3], 1), 0, SECT - 1).astype(jnp.int32),
        "active": place_ends((jax.random.randint(splits[4], (SEGS, TERMS, SECT), 0, 2) < 1).astype(jnp.int32), jax.random.fold_in(splits[4], 1), 0, 1),
    }


precise = lax.Precision.HIGHEST
step_size = 0.3

def blockmul(left, right):
    return jnp.einsum('sij,sjl->sil', left, right, precision=precise)

def gram_blocks(piece):
    wide = piece.astype(jnp.float32)
    return jnp.einsum('sji,sjl->sil', wide, wide, precision=precise)

def term_parts(state_low, left_k, right_k):
    half = jnp.einsum('sij,sjl->sil', left_k.astype(jnp.float32), state_low.astype(jnp.float32), precision=precise).astype(jnp.bfloat16)
    return jnp.einsum('sil,sml->sim', half.astype(jnp.float32), right_k.astype(jnp.float32), precision=precise)

def term_sum(state_low, lefts, rights, weights, shift_list):

    def add_term(running, items):
        left_k, right_k, weight_k, shift_k = items
        placed = weight_k[:, None, None] * term_parts(state_low, left_k, right_k)
        return (running + jnp.roll(placed, shift_k, axis=0), None)
    start_sum = jnp.zeros((SECT, QB, QB), jnp.float32)
    summed, _ = lax.scan(add_term, start_sum, (lefts, rights, weights, shift_list))
    return summed * (1.0 / TERMS)

def term_values(state_low, lefts, rights, weights, shift_list):
    wide_low = state_low.astype(jnp.float32)

    def one_term(carried, items):
        left_k, right_k, weight_k, shift_k = items
        target = jnp.roll(wide_low, -shift_k, axis=0)
        per_block = lax.optimization_barrier(jnp.sum(term_parts(state_low, left_k, right_k) * target, axis=(1, 2)))
        return (carried, jnp.sum(weight_k * per_block) * (1.0 / (SECT * QB * QB)))
    _, values = lax.scan(one_term, jnp.zeros((), jnp.float32), (lefts, rights, weights, shift_list))
    return values

def reference(psi_start, left_ops, right_ops, shifts, active):
    count = float(SECT * QB * QB)
    states = [psi_start[seg_index].astype(jnp.float32) for seg_index in range(N_SEG)]
    for sweep_index in range(ITERS):
        lows = [current.astype(jnp.bfloat16) for current in states]
        updated = []
        for seg_index in range(N_SEG):
            current = states[seg_index]
            env = jnp.zeros((SECT, QB, QB), jnp.float32)
            if seg_index > 0:
                env = env + gram_blocks(lows[seg_index - 1])
            if seg_index < N_SEG - 1:
                env = env + gram_blocks(lows[seg_index + 1])
            weights = active[seg_index].astype(jnp.float32)
            applied = term_sum(lows[seg_index], left_ops[seg_index], right_ops[seg_index], weights, shifts[seg_index]) + blockmul(current, env) * (0.5 / QB)
            rho = jnp.sum(current * applied) / jnp.sum(current * current)
            stepped = current - step_size * (applied - rho * current)
            updated.append(stepped * jnp.sqrt(count / jnp.sum(stepped * stepped)))
        states = updated
    finals = [current.astype(jnp.bfloat16) for current in states]
    values = []
    for seg_index in range(N_SEG):
        weights = active[seg_index].astype(jnp.float32)
        values.append(term_values(finals[seg_index], left_ops[seg_index], right_ops[seg_index], weights, shifts[seg_index]))
    return (jnp.stack(finals), jnp.stack(values))
```

```python
import functools

import jax
import jax.numpy as jnp
from jax import lax
from jax.experimental import pallas as pl
from jax.experimental.pallas import tpu as pltpu
from jax.sharding import PartitionSpec as P

ITERS = 3
STEP = 0.3
MESH = pl.DeviceIdType.MESH
F32 = jnp.float32
BF16 = jnp.bfloat16


def kernel(
    nz, nx, nseg, axis_terms,
    psi_ref, left_hbm, right_hbm, shift_ref, active_ref,
    state_ref, rdm_ref,
    left_v, right_v, half_v, ag, xsend, xrecv, own_acc, zsend, zrecv,
    scz, scx, nbr, cur_v, tcur_v, app_v,
    load_sem, ag_zs, ag_zr, ag_xs, ag_xr, rs_xs, rs_xr, rs_zs, rs_zr,
    sc_zs, sc_zr, sc_xs, sc_xr, nb_s, nb_r,
):
    terms, blocks, width = left_v.shape[0], left_v.shape[1], left_v.shape[2]
    count = float(blocks * width * width)
    term_scale = 1.0 / (terms * axis_terms)
    seg = lax.axis_index("seg")
    me = lax.axis_index("op")
    z, x = me // nx, me % nx

    def device(zz, xx):
        return (seg, zz * nx + xx)

    def remote(src, dst, send_sem, recv_sem, where):
        return pltpu.make_async_remote_copy(
            src_ref=src, dst_ref=dst, send_sem=send_sem, recv_sem=recv_sem,
            device_id=where, device_id_type=MESH,
        )

    def near_first(i):
        hop = i // 2 + 1
        return hop + (i % 2) * (nz - 2 * hop)

    left_load = pltpu.make_async_copy(left_hbm, left_v, load_sem.at[0])
    right_load = pltpu.make_async_copy(right_hbm, right_v, load_sem.at[1])
    left_load.start()
    right_load.start()

    seg_up = (seg + 1) % nseg
    seg_down = (seg + nseg - 1) % nseg
    barrier = pltpu.get_barrier_semaphore()
    for dz in range(1, nz):
        pl.semaphore_signal(barrier, inc=1, device_id=device((z + dz) % nz, x), device_id_type=MESH)
    for dx in range(1, nx):
        pl.semaphore_signal(barrier, inc=1, device_id=device(z, (x + dx) % nx), device_id_type=MESH)
    for other in (seg_up, seg_down):
        pl.semaphore_signal(barrier, inc=1, device_id=(other, me), device_id_type=MESH)
    pl.semaphore_wait(barrier, nz - 1 + nx - 1 + 2)

    def gather_z(p, dz):
        return remote(ag.at[p, z, x], ag.at[p, z, x], ag_zs.at[p, dz], ag_zr.at[p, dz],
                      device((z + dz) % nz, x))

    def gather_z_in(p, dz):
        block = ag.at[p, (z + nz - dz) % nz, x]
        return remote(block, block, ag_zs.at[p, dz], ag_zr.at[p, dz], device((z + dz) % nz, x))

    def gather_x(p, dz, dx):
        block = ag.at[p, (z + nz - dz) % nz, x]
        return remote(block, block, ag_xs.at[p, dz, dx], ag_xr.at[p, dz, dx], device(z, (x + dx) % nx))

    def gather_x_in(p, dz, dx):
        block = ag.at[p, (z + nz - dz) % nz, (x + nx - dx) % nx]
        return remote(block, block, ag_xs.at[p, dz, dx], ag_xr.at[p, dz, dx], device(z, (x + dx) % nx))

    def gather_start(p):
        for i in reversed(range(nz - 1)):
            gather_z(p, near_first(i)).start()
        for dx in range(1, nx):
            gather_x(p, 0, dx).start()

    def half_block(p, bz, bx):
        s = bz * nx + bx
        stacked = left_v[:, s].reshape(terms * width, width)
        half = jnp.dot(stacked, ag[p, bz, bx], preferred_element_type=F32)
        for k in range(terms):
            weight = active_ref[k, s].astype(F32)
            half_v[k, s] = (half[k * width:(k + 1) * width] * weight).astype(BF16)

    def gather_column(p):
        def arrive(i, carry):
            dz = near_first(i)
            gather_z_in(p, dz).wait_recv()
            for dx in range(1, nx):
                gather_x(p, dz, dx).start()
            half_block(p, (z + nz - dz) % nz, x)
            return carry
        half_block(p, z, x)
        lax.fori_loop(0, nz - 1, arrive, 0)

    def gather_rest(p):
        def row(i, carry):
            dz = i
            for dx in range(1, nx):
                gather_x_in(p, dz, dx).wait_recv()
                half_block(p, (z + nz - dz) % nz, (x + nx - dx) % nx)
            return carry
        lax.fori_loop(0, nz, row, 0)

    def gathered(t):
        halves, rights = [], []
        for k in range(terms):
            s = lax.rem(t + blocks - shift_ref[k], blocks)
            halves.append(half_v[k, s])
            rights.append(right_v[k, s])
        return jnp.concatenate(halves, axis=1), jnp.concatenate(rights, axis=1)

    def term_block(t):
        halves, rights = gathered(t)
        return lax.dot_general(halves, rights, (((1,), (1,)), ((), ())), preferred_element_type=F32)

    def scatter_x(q, dz, dx):
        return remote(xsend.at[q, dz, dx - 1], xrecv.at[q, dz, dx - 1], rs_xs.at[q, dz, dx],
                      rs_xr.at[q, dz, dx], device(z, (x + dx) % nx))

    def scatter_z(q, dz):
        return remote(zsend.at[q, dz], zrecv.at[q, dz], rs_zs.at[q, dz], rs_zr.at[q, dz],
                      device((z + dz) % nz, x))

    def scatter_send(q):
        def row(i, carry):
            dz = nz - 1 - i
            base = ((z + dz) % nz) * nx
            for dx in range(1, nx):
                xsend[q, dz, dx - 1] = term_block(base + (x + dx) % nx).astype(BF16)
                scatter_x(q, dz, dx).start()
            own_acc[dz] = term_block(base + x)
            return carry
        lax.fori_loop(0, nz, row, 0)

    def column_sum(q, dz):
        total = own_acc[dz]
        for dx in range(1, nx):
            scatter_x(q, dz, dx).wait_recv()
            total = total + xrecv[q, dz, dx - 1].astype(F32)
        return total

    def scatter_finish(q):
        def row(i, carry):
            dz = nz - 1 - i
            zsend[q, dz] = column_sum(q, dz).astype(BF16)
            scatter_z(q, dz).start()
            return carry
        lax.fori_loop(0, nz - 1, row, 0)
        total = column_sum(q, 0)
        for dz in range(1, nz):
            scatter_z(q, dz).wait_recv()
            total = total + zrecv[q, dz].astype(F32)
        return total * term_scale

    def scalars_z(q, dz):
        return remote(scz.at[q, z], scz.at[q, z], sc_zs.at[q, dz], sc_zr.at[q, dz],
                      device((z + dz) % nz, x))

    def scalars_x(q, dx):
        return remote(scx.at[q, x], scx.at[q, x], sc_xs.at[q, dx], sc_xr.at[q, dx],
                      device(z, (x + dx) % nx))

    def scalars_start(q, cur, applied):
        rows = lax.broadcasted_iota(jnp.int32, (8, width), 0)
        a = jnp.sum(cur * applied)
        b = jnp.sum(cur * cur)
        c = jnp.sum(applied * applied)
        scz[q, z] = jnp.where(rows == 0, a, jnp.where(rows == 1, b, c))
        for dz in range(1, nz):
            scalars_z(q, dz).start()

    def scalars_middle(q):
        for dz in range(1, nz):
            scalars_z(q, dz).wait_recv()
        total = scz[q, 0]
        for zz in range(1, nz):
            total = total + scz[q, zz]
        scx[q, x] = total
        for dx in range(1, nx):
            scalars_x(q, dx).start()

    def scalars_end(q):
        for dx in range(1, nx):
            scalars_x(q, dx).wait_recv()
        total = scx[q, 0]
        for xx in range(1, nx):
            total = total + scx[q, xx]
        a, b, c = total[0:1], total[1:2], total[2:3]
        rho = a / b
        norm = b + (STEP * STEP) * jnp.maximum(c - a * rho, 0.0)
        scale = jnp.sqrt(count / norm)
        return scale * (1.0 + STEP * rho), scale * STEP

    def neighbours(n):
        up = remote(nbr.at[n, 2], nbr.at[n, 0], nb_s.at[n, 0], nb_r.at[n, 0], (seg_up, me))
        down = remote(nbr.at[n, 2], nbr.at[n, 1], nb_s.at[n, 1], nb_r.at[n, 1], (seg_down, me))
        return up, down

    def neighbours_start(n, low):
        nbr[n, 2] = low
        for copy in neighbours(n):
            copy.start()

    has_left = (seg > 0).astype(F32)
    has_right = (seg < nseg - 1).astype(F32)

    def environment(n, cur):
        for copy in neighbours(n):
            copy.wait_recv()
        first = (nbr[n, 0].astype(F32) * has_left).astype(BF16)
        second = (nbr[n, 1].astype(F32) * has_right).astype(BF16)
        both = jnp.concatenate([first, second], axis=0)
        env = lax.dot_general(both, both, (((0,), (0,)), ((), ())), preferred_element_type=F32)
        return jnp.dot(cur, env, precision=lax.Precision.HIGHEST, preferred_element_type=F32) * (0.5 / width)

    start = psi_ref[0, 0]
    ag[0, z, x] = start
    gather_start(0)
    neighbours_start(0, start)
    cur_v[...] = start.astype(F32)
    left_load.wait()
    right_load.wait()

    for n in range(ITERS):
        gather_column(n)
        if n > 0:
            scalars_middle(n - 1)
        gather_rest(n)
        if n > 0:
            keep, take = scalars_end(n - 1)
            cur_v[...] = keep * cur_v[...] - take * app_v[...]
            neighbours_start(n, cur_v[...].astype(BF16))
        scatter_send(n)
        env_part = environment(n, cur_v[...])
        total = scatter_finish(n)
        if n > 0:
            total = keep * tcur_v[...] - take * total
        tcur_v[...] = total
        applied = total + env_part
        app_v[...] = applied
        if n < ITERS - 1:
            ag[n + 1, z, x] = applied.astype(BF16)
            gather_start(n + 1)
        scalars_start(n, cur_v[...], applied)

    scalars_middle(ITERS - 1)
    keep, take = scalars_end(ITERS - 1)
    final = (keep * cur_v[...] - take * app_v[...]).astype(BF16)
    ag[ITERS, z, x] = final
    gather_start(ITERS)
    state_ref[0, 0] = final
    gather_column(ITERS)
    gather_rest(ITERS)

    def values(t, acc):
        halves, rights = gathered(t)
        crossed = jnp.dot(ag[ITERS, t // nx, t % nx], rights, preferred_element_type=F32)
        crossed = crossed * halves.astype(F32)
        return acc + jnp.sum(crossed.reshape(width // 8, 8, terms * width), axis=0)

    acc = lax.fori_loop(0, blocks, values, jnp.zeros((8, terms * width), F32))
    for k in range(terms):
        rdm_ref[0, k] = jnp.sum(acc[:, k * width:(k + 1) * width]) * (1.0 / count)

    def drain_gather(p, carry):
        for dz in range(1, nz):
            gather_z(p, dz).wait_send()
        for dz in range(nz):
            for dx in range(1, nx):
                gather_x(p, dz, dx).wait_send()
        return carry

    lax.fori_loop(0, ITERS + 1, drain_gather, 0)

    def drain_iter(n, carry):
        for dz in range(nz):
            for dx in range(1, nx):
                scatter_x(n, dz, dx).wait_send()
        for dz in range(1, nz):
            scatter_z(n, dz).wait_send()
            scalars_z(n, dz).wait_send()
        for dx in range(1, nx):
            scalars_x(n, dx).wait_send()
        for copy in neighbours(n):
            copy.wait_send()
        return carry

    lax.fori_loop(0, ITERS, drain_iter, 0)


def shards(nseg, nop, psi_start, left_ops, right_ops, shifts, active):
    nx = 4 if nop == 32 else 2
    nz = nop // nx
    terms, blocks, width = left_ops.shape[1], left_ops.shape[2], left_ops.shape[3]
    vmem, dma = pltpu.VMEM, pltpu.SemaphoreType.DMA
    tile = (width, width)
    return pl.pallas_call(
        functools.partial(kernel, nz, nx, nseg, nop),
        out_shape=(
            jax.ShapeDtypeStruct((1, 1) + tile, BF16),
            jax.ShapeDtypeStruct((1, terms), F32),
        ),
        in_specs=[
            pl.BlockSpec(memory_space=pltpu.VMEM),
            pl.BlockSpec(memory_space=pl.ANY),
            pl.BlockSpec(memory_space=pl.ANY),
            pl.BlockSpec(memory_space=pltpu.SMEM),
            pl.BlockSpec(memory_space=pltpu.SMEM),
        ],
        out_specs=(
            pl.BlockSpec(memory_space=pltpu.VMEM),
            pl.BlockSpec(memory_space=pltpu.SMEM),
        ),
        scratch_shapes=[
            vmem((terms, blocks) + tile, BF16),
            vmem((terms, blocks) + tile, BF16),
            vmem((terms, blocks) + tile, BF16),
            vmem((ITERS + 1, nz, nx) + tile, BF16),
            vmem((ITERS, nz, nx - 1) + tile, BF16),
            vmem((ITERS, nz, nx - 1) + tile, BF16),
            vmem((nz,) + tile, F32),
            vmem((ITERS, nz) + tile, BF16),
            vmem((ITERS, nz) + tile, BF16),
            vmem((ITERS, nz, 8, width), F32),
            vmem((ITERS, nx, 8, width), F32),
            vmem((ITERS, 3) + tile, BF16),
            vmem(tile, F32),
            vmem(tile, F32),
            vmem(tile, F32),
            dma((2,)),
            dma((ITERS + 1, nz)),
            dma((ITERS + 1, nz)),
            dma((ITERS + 1, nz, nx)),
            dma((ITERS + 1, nz, nx)),
            dma((ITERS, nz, nx)),
            dma((ITERS, nz, nx)),
            dma((ITERS, nz)),
            dma((ITERS, nz)),
            dma((ITERS, nz)),
            dma((ITERS, nz)),
            dma((ITERS, nx)),
            dma((ITERS, nx)),
            dma((ITERS, 2)),
            dma((ITERS, 2)),
        ],
        compiler_params=pltpu.CompilerParams(
            collective_id=0, has_side_effects=True, vmem_limit_bytes=48 * 1024 * 1024
        ),
        name="chain",
    )(
        psi_start,
        left_ops.reshape(left_ops.shape[1:]),
        right_ops.reshape(right_ops.shape[1:]),
        shifts.reshape(terms),
        active.reshape(terms, blocks),
    )


def solution(mesh):
    return jax.shard_map(
        functools.partial(shards, mesh.shape["seg"], mesh.shape["op"]),
        mesh=mesh,
        in_specs=(
            P("seg", "op", None, None),
            P("seg", "op", None, None, None),
            P("seg", "op", None, None, None),
            P("seg", "op"),
            P("seg", "op", None),
        ),
        out_specs=(P("seg", "op", None, None), P("seg", "op")),
        check_vma=False,
    )
```

```python
import functools

import jax
import jax.numpy as jnp
from jax import lax
from jax.experimental import pallas as pl
from jax.experimental.pallas import tpu as pltpu
from jax.sharding import PartitionSpec as P

ITERS = 3
STEP = 0.3
MESH = pl.DeviceIdType.MESH
F32 = jnp.float32
BF16 = jnp.bfloat16


def kernel(
    nz, nx, nseg, axis_terms,
    psi_hbm, left_hbm, right_hbm, shift_ref, active_ref,
    state_ref, rdm_ref,
    psi_v, left_v, right_v, half_v, ag, xsend, xrecv, own_acc, zsend, zrecv,
    scz, scx, nbr, cur_v, tcur_v, app_v,
    load_sem, ag_zs, ag_zr, ag_xs, ag_xr, rs_xs, rs_xr, rs_zs, rs_zr,
    sc_zs, sc_zr, sc_xs, sc_xr, nb_s, nb_r,
):
    terms, blocks, width = left_v.shape[0], left_v.shape[1], left_v.shape[2]
    count = float(blocks * width * width)
    term_scale = 1.0 / (terms * axis_terms)
    others = nx - 1
    seg = lax.axis_index("seg")
    me = lax.axis_index("op")
    z, x = me // nx, me % nx
    x_order = (1, 3, 2) if nx == 4 else (1,)

    def device(dz, dx):
        return (seg, ((z + dz) % nz) * nx + (x + dx) % nx)

    def slot(dz, dx):
        return ((z + nz - dz) % nz) * nx + (x + nx - dx) % nx

    def remote(src, dst, send_sem, recv_sem, where):
        return pltpu.make_async_remote_copy(
            src_ref=src, dst_ref=dst, send_sem=send_sem, recv_sem=recv_sem,
            device_id=where, device_id_type=MESH,
        )

    def near_first(i):
        hop = (i + 1) // 2
        return (hop + ((i + 1) % 2) * (nz - 2 * hop)) % nz

    psi_load = pltpu.make_async_copy(psi_hbm.at[0, 0], psi_v, load_sem.at[0])
    left_load = pltpu.make_async_copy(left_hbm, left_v, load_sem.at[1])
    right_load = pltpu.make_async_copy(right_hbm, right_v, load_sem.at[2])
    psi_load.start()
    left_load.start()
    right_load.start()

    seg_up = (seg + 1) % nseg
    seg_down = (seg + nseg - 1) % nseg
    barrier = pltpu.get_barrier_semaphore()
    for dz in range(1, nz):
        pl.semaphore_signal(barrier, inc=1, device_id=device(dz, 0), device_id_type=MESH)
    for dx in range(1, nx):
        pl.semaphore_signal(barrier, inc=1, device_id=device(0, dx), device_id_type=MESH)
    for other in (seg_up, seg_down):
        pl.semaphore_signal(barrier, inc=1, device_id=(other, me), device_id_type=MESH)
    psi_load.wait()
    start = psi_v[...]
    ag[0, me] = start
    nbr[0, 2] = start
    cur_v[...] = start.astype(F32)
    pl.semaphore_wait(barrier, nz - 1 + nx - 1 + 2)

    def gather_z(p, dz):
        return remote(ag.at[p, me], ag.at[p, me], ag_zs.at[p], ag_zr.at[p, dz], device(dz, 0))

    def gather_x(p, dz, dx):
        block = ag.at[p, slot(dz, 0)]
        return remote(block, block, ag_xs.at[p], ag_xr.at[p, dz], device(0, dx))

    def gather_start(p):
        for i in range(1, nz):
            gather_z(p, near_first(i)).start()
            if i == min(2, nz - 1):
                for dx in x_order:
                    gather_x(p, 0, dx).start()

    def half_row(p, dz):
        stacked = []
        for dx in range(nx):
            s = slot(dz, dx)
            ops = left_v[:, s].reshape(terms * width, width)
            stacked.append((s, jnp.dot(ops, ag[p, s], preferred_element_type=F32)))
        for s, half in stacked:
            for k in range(terms):
                weight = active_ref[k, s].astype(F32)
                half_v[k, s] = (half[k * width:(k + 1) * width] * weight).astype(BF16)

    def gather_column(p):
        def arrive(i, carry):
            dz = near_first(i)
            block = ag.at[p, slot(dz, 0)]
            remote(block, block, ag_zs.at[p], ag_zr.at[p, dz], device(dz, 0)).wait_recv()
            for dx in x_order:
                gather_x(p, dz, dx).start()
            return carry
        lax.fori_loop(1, nz, arrive, 0)

    def gather_rest(p):
        def row(i, carry):
            dz = near_first(i)
            three = ag.at[p, pl.ds(0, others)]
            remote(three, three, ag_xs.at[p], ag_xr.at[p, dz], device(0, 1)).wait_recv()
            half_row(p, dz)
            return carry
        lax.fori_loop(0, nz, row, 0)

    def gathered(t):
        halves, rights = [], []
        for k in range(terms):
            s = lax.rem(t + blocks - shift_ref[k], blocks)
            halves.append(half_v[k, s])
            rights.append(right_v[k, s])
        return jnp.concatenate(halves, axis=1), jnp.concatenate(rights, axis=1)

    def term_block(t):
        halves, rights = gathered(t)
        return lax.dot_general(halves, rights, (((1,), (1,)), ((), ())), preferred_element_type=F32)

    def scatter_x(q, dz, dx):
        place = dz * others + dx - 1
        return remote(xsend.at[q, place], xrecv.at[q, place], rs_xs.at[q], rs_xr.at[q, dz], device(0, dx))

    def scatter_z(q, dz):
        return remote(zsend.at[q, dz - 1], zrecv.at[q, dz - 1], rs_zs.at[q], rs_zr.at[q], device(dz, 0))

    def scatter_send(q):
        def row(i, carry):
            dz = near_first(nz - 1 - i)
            base = ((z + dz) % nz) * nx
            parts = [term_block(base + (x + dx) % nx) for dx in range(nx)]
            own_acc[dz] = parts[0]
            for dx in x_order:
                xsend[q, dz * others + dx - 1] = parts[dx].astype(BF16)
            for dx in x_order:
                scatter_x(q, dz, dx).start()
            return carry
        lax.fori_loop(0, nz, row, 0)

    def column_sum(q, dz):
        three = pl.ds(dz * others, others)
        remote(xsend.at[q, three], xrecv.at[q, three], rs_xs.at[q], rs_xr.at[q, dz], device(0, 1)).wait_recv()
        total = own_acc[dz]
        for dx in range(1, nx):
            total = total + xrecv[q, dz * others + dx - 1].astype(F32)
        return total

    def scatter_finish(q):
        def row(i, carry):
            dz = near_first(nz - 1 - i)
            zsend[q, dz - 1] = column_sum(q, dz).astype(BF16)
            scatter_z(q, dz).start()
            return carry
        lax.fori_loop(0, nz - 1, row, 0)
        total = column_sum(q, 0)
        remote(zsend.at[q], zrecv.at[q], rs_zs.at[q], rs_zr.at[q], device(1, 0)).wait_recv()
        for dz in range(1, nz):
            total = total + zrecv[q, dz - 1].astype(F32)
        return total * term_scale

    def scalars_z(q, dz):
        return remote(scz.at[q, z], scz.at[q, z], sc_zs.at[q], sc_zr.at[q], device(dz, 0))

    def scalars_x(q, dx):
        return remote(scx.at[q, x], scx.at[q, x], sc_xs.at[q], sc_xr.at[q], device(0, dx))

    def scalars_start(q, cur, applied):
        rows = lax.broadcasted_iota(jnp.int32, (8, width), 0)
        a = jnp.sum(cur * applied)
        b = jnp.sum(cur * cur)
        c = jnp.sum(applied * applied)
        scz[q, z] = jnp.where(rows == 0, a, jnp.where(rows == 1, b, c))
        for i in range(1, nz):
            scalars_z(q, near_first(nz - i)).start()

    def scalars_middle(q):
        many = scz.at[q, pl.ds(0, nz - 1)]
        remote(many, many, sc_zs.at[q], sc_zr.at[q], device(1, 0)).wait_recv()
        total = scz[q, 0]
        for zz in range(1, nz):
            total = total + scz[q, zz]
        scx[q, x] = total
        for dx in range(1, nx):
            scalars_x(q, dx).start()

    def scalars_end(q):
        many = scx.at[q, pl.ds(0, others)]
        remote(many, many, sc_xs.at[q], sc_xr.at[q], device(0, 1)).wait_recv()
        total = scx[q, 0]
        for xx in range(1, nx):
            total = total + scx[q, xx]
        a, b, c = total[0:1], total[1:2], total[2:3]
        rho = a / b
        norm = b + (STEP * STEP) * jnp.maximum(c - a * rho, 0.0)
        scale = jnp.sqrt(count / norm)
        return scale * (1.0 + STEP * rho), scale * STEP

    def neighbours(n):
        up = remote(nbr.at[n, 2], nbr.at[n, 0], nb_s.at[n, 0], nb_r.at[n, 0], (seg_up, me))
        down = remote(nbr.at[n, 2], nbr.at[n, 1], nb_s.at[n, 1], nb_r.at[n, 1], (seg_down, me))
        return up, down

    has_left = (seg > 0).astype(F32)
    has_right = (seg < nseg - 1).astype(F32)

    def environment(n, cur):
        for copy in neighbours(n):
            copy.wait_recv()
        first = (nbr[n, 0].astype(F32) * has_left).astype(BF16)
        second = (nbr[n, 1].astype(F32) * has_right).astype(BF16)
        both = jnp.concatenate([first, second], axis=0)
        env = lax.dot_general(both, both, (((0,), (0,)), ((), ())), preferred_element_type=F32)
        return jnp.dot(cur, env, precision=lax.Precision.HIGHEST, preferred_element_type=F32) * (0.5 / width)

    gather_start(0)
    for copy in neighbours(0):
        copy.start()

    for n in range(ITERS):
        gather_column(n)
        if n == 0:
            left_load.wait()
            right_load.wait()
        else:
            scalars_middle(n - 1)
        gather_rest(n)
        scatter_send(n)
        if n > 0:
            keep, take = scalars_end(n - 1)
            cur = keep * cur_v[...] - take * app_v[...]
            cur_v[...] = cur
            nbr[n, 2] = cur.astype(BF16)
            for copy in neighbours(n):
                copy.start()
            tcur_v[...] = keep * tcur_v[...]
        app_v[...] = environment(n, cur_v[...])
        total = scatter_finish(n)
        if n > 0:
            total = tcur_v[...] - take * total
        applied = total + app_v[...]
        if n < ITERS - 1:
            ag[n + 1, me] = applied.astype(BF16)
            gather_start(n + 1)
        tcur_v[...] = total
        app_v[...] = applied
        scalars_start(n, cur_v[...], applied)

    scalars_middle(ITERS - 1)
    keep, take = scalars_end(ITERS - 1)
    final = (keep * cur_v[...] - take * app_v[...]).astype(BF16)
    ag[ITERS, me] = final
    gather_start(ITERS)
    state_ref[0, 0] = final
    gather_column(ITERS)
    gather_rest(ITERS)

    def values(t, acc):
        halves, rights = gathered(t)
        crossed = jnp.dot(ag[ITERS, t], rights, preferred_element_type=F32)
        crossed = crossed * halves.astype(F32)
        return acc + jnp.sum(crossed.reshape(width // 8, 8, terms * width), axis=0)

    acc = lax.fori_loop(0, blocks, values, jnp.zeros((8, terms * width), F32), unroll=4)
    for k in range(terms):
        rdm_ref[0, k] = jnp.sum(acc[:, k * width:(k + 1) * width]) * (1.0 / count)

    for p in range(ITERS + 1):
        column = ag.at[p, pl.ds(0, nz - 1)]
        rest = ag.at[p, pl.ds(0, nz * others)]
        remote(column, column, ag_zs.at[p], ag_zr.at[p, 0], device(1, 0)).wait_send()
        remote(rest, rest, ag_xs.at[p], ag_xr.at[p, 0], device(0, 1)).wait_send()
    for n in range(ITERS):
        remote(xsend.at[n], xrecv.at[n], rs_xs.at[n], rs_xr.at[n, 0], device(0, 1)).wait_send()
        remote(zsend.at[n], zrecv.at[n], rs_zs.at[n], rs_zr.at[n], device(1, 0)).wait_send()
        many = scz.at[n, pl.ds(0, nz - 1)]
        remote(many, many, sc_zs.at[n], sc_zr.at[n], device(1, 0)).wait_send()
        many = scx.at[n, pl.ds(0, others)]
        remote(many, many, sc_xs.at[n], sc_xr.at[n], device(0, 1)).wait_send()
        for copy in neighbours(n):
            copy.wait_send()


def shards(nseg, nop, psi_start, left_ops, right_ops, shifts, active):
    nx = 4 if nop == 32 else 2
    nz = nop // nx
    terms, blocks, width = left_ops.shape[1], left_ops.shape[2], left_ops.shape[3]
    vmem, dma = pltpu.VMEM, pltpu.SemaphoreType.DMA
    tile = (width, width)
    return pl.pallas_call(
        functools.partial(kernel, nz, nx, nseg, nop),
        out_shape=(
            jax.ShapeDtypeStruct((1, 1) + tile, BF16),
            jax.ShapeDtypeStruct((1, terms), F32),
        ),
        in_specs=[
            pl.BlockSpec(memory_space=pltpu.HBM),
            pl.BlockSpec(memory_space=pltpu.HBM),
            pl.BlockSpec(memory_space=pltpu.HBM),
            pl.BlockSpec(memory_space=pltpu.SMEM),
            pl.BlockSpec(memory_space=pltpu.SMEM),
        ],
        out_specs=(
            pl.BlockSpec(memory_space=pltpu.VMEM),
            pl.BlockSpec(memory_space=pltpu.SMEM),
        ),
        scratch_shapes=[
            vmem(tile, BF16),
            vmem((terms, blocks) + tile, BF16),
            vmem((terms, blocks) + tile, BF16),
            vmem((terms, blocks) + tile, BF16),
            vmem((ITERS + 1, nop) + tile, BF16),
            vmem((ITERS, nz * (nx - 1)) + tile, BF16),
            vmem((ITERS, nz * (nx - 1)) + tile, BF16),
            vmem((nz,) + tile, F32),
            vmem((ITERS, nz - 1) + tile, BF16),
            vmem((ITERS, nz - 1) + tile, BF16),
            vmem((ITERS, nz, 8, width), F32),
            vmem((ITERS, nx, 8, width), F32),
            vmem((ITERS, 3) + tile, BF16),
            vmem(tile, F32),
            vmem(tile, F32),
            vmem(tile, F32),
            dma((3,)),
            dma((ITERS + 1,)),
            dma((ITERS + 1, nz)),
            dma((ITERS + 1,)),
            dma((ITERS + 1, nz)),
            dma((ITERS,)),
            dma((ITERS, nz)),
            dma((ITERS,)),
            dma((ITERS,)),
            dma((ITERS,)),
            dma((ITERS,)),
            dma((ITERS,)),
            dma((ITERS,)),
            dma((ITERS, 2)),
            dma((ITERS, 2)),
        ],
        compiler_params=pltpu.CompilerParams(
            collective_id=0, has_side_effects=True, vmem_limit_bytes=63 * 1024 * 1024
        ),
        name="chain",
    )(
        psi_start,
        left_ops.reshape(left_ops.shape[1:]),
        right_ops.reshape(right_ops.shape[1:]),
        shifts.reshape(terms),
        active.reshape(terms, blocks),
    )


def solution(mesh):
    return jax.shard_map(
        functools.partial(shards, mesh.shape["seg"], mesh.shape["op"]),
        mesh=mesh,
        in_specs=(
            P("seg", "op", None, None),
            P("seg", "op", None, None, None),
            P("seg", "op", None, None, None),
            P("seg", "op"),
            P("seg", "op", None),
        ),
        out_specs=(P("seg", "op", None, None), P("seg", "op")),
        check_vma=False,
    )
```

```python
import functools

import jax
import jax.numpy as jnp
from jax import lax
from jax.experimental import pallas as pl
from jax.experimental.pallas import tpu as pltpu
from jax.sharding import PartitionSpec as P

ITERS = 3
STEP = 0.3
MESH = pl.DeviceIdType.MESH
F32 = jnp.float32
BF16 = jnp.bfloat16


TREE = (
    ((1, 0), (0, 0)), ((7, 0), (0, 0)), ((0, 1), (0, 0)), ((0, 3), (0, 0)),
    ((0, 2), (0, 0)), ((2, 0), (0, 0)), ((6, 0), (0, 0)), ((1, 1), (1, 0)),
    ((1, 3), (1, 0)), ((2, 1), (1, 0)), ((1, 2), (0, 2)), ((7, 2), (7, 0)),
    ((2, 3), (2, 0)), ((4, 0), (7, 0)), ((6, 1), (6, 0)), ((6, 3), (6, 0)),
    ((5, 3), (6, 0)), ((3, 2), (0, 2)), ((2, 2), (2, 1)), ((7, 1), (1, 1)),
    ((3, 1), (2, 1)), ((7, 3), (7, 2)), ((4, 3), (4, 0)), ((3, 0), (4, 0)),
    ((3, 3), (2, 3)), ((4, 1), (4, 0)), ((6, 2), (6, 3)), ((5, 1), (6, 1)),
    ((5, 0), (5, 3)), ((4, 2), (3, 2)), ((5, 2), (5, 3)),
)


def gather_tree(nz, nx):
    if (nz, nx) == (8, 4):
        tree = TREE
    else:
        tree = tuple(((dz, 0), (0, 0)) for dz in range(1, nz))
        tree += tuple(((dz, dx), (dz, 0)) for dz in range(nz) for dx in range(1, nx))
    kids = {}
    for child, parent in tree:
        kids.setdefault(parent, []).append(child)

    def hops(child, parent):
        up, right = (child[0] - parent[0]) % nz, (child[1] - parent[1]) % nx
        return min(up, nz - up) + min(right, nx - right)

    for parent, children in kids.items():
        children.sort(key=lambda child: (hops(child, parent), -len(kids.get(child, ()))))
    return [child for child, _ in tree], kids


def kernel(
    nz, nx, nseg, axis_terms,
    psi_hbm, left_hbm, right_hbm, shift_hbm, active_hbm,
    state_hbm, rdm_ref,
    psi_v, shift_ref, active_ref, left_v, right_v, half_v, ag, xsend, xrecv, own_acc, zsend, zrecv,
    scz, scx, nbr, cur_v, tcur_v, app_v,
    load_sem, ag_s, ag_r, rs_xs, rs_xr, rs_zs, rs_zr,
    sc_zs, sc_zr, sc_xs, sc_xr, nb_s, nb_r,
):
    terms, blocks, width = left_v.shape[0], left_v.shape[1], left_v.shape[2]
    count = float(blocks * width * width)
    term_scale = 1.0 / (terms * axis_terms)
    others = nx - 1
    seg = lax.axis_index("seg")
    me = lax.axis_index("op")
    z, x = me // nx, me % nx
    x_order = (1, 3, 2) if nx == 4 else (1,)

    def device(dz, dx):
        return (seg, ((z + dz) % nz) * nx + (x + dx) % nx)

    def slot(dz, dx):
        return ((z + nz - dz) % nz) * nx + (x + nx - dx) % nx

    def remote(src, dst, send_sem, recv_sem, where):
        return pltpu.make_async_remote_copy(
            src_ref=src, dst_ref=dst, send_sem=send_sem, recv_sem=recv_sem,
            device_id=where, device_id_type=MESH,
        )

    def near_first(i):
        hop = (i + 1) // 2
        return (hop + ((i + 1) % 2) * (nz - 2 * hop)) % nz

    psi_load = pltpu.make_async_copy(psi_hbm.at[0, 0], psi_v, load_sem.at[0])
    left_load = pltpu.make_async_copy(left_hbm, left_v, load_sem.at[1])
    right_load = pltpu.make_async_copy(right_hbm, right_v, load_sem.at[2])
    psi_load.start()
    shift_load = pltpu.make_async_copy(shift_hbm, shift_ref, load_sem.at[3])
    active_load = pltpu.make_async_copy(active_hbm, active_ref, load_sem.at[4])
    left_load.start()
    right_load.start()
    shift_load.start()
    active_load.start()

    seg_up = (seg + 1) % nseg
    seg_down = (seg + nseg - 1) % nseg
    order, kids = gather_tree(nz, nx)
    steps = {((c[0] - p[0]) % nz, (c[1] - p[1]) % nx) for p in kids for c in kids[p]}
    steps |= {(dz, 0) for dz in range(1, nz)} | {(0, dx) for dx in range(1, nx)}
    steps |= {((nz - dz) % nz, (nx - dx) % nx) for dz, dx in steps}
    barrier = pltpu.get_barrier_semaphore()
    for dz, dx in sorted(steps):
        pl.semaphore_signal(barrier, inc=1, device_id=device(dz, dx), device_id_type=MESH)
    for other in (seg_up, seg_down):
        pl.semaphore_signal(barrier, inc=1, device_id=(other, me), device_id_type=MESH)
    psi_load.wait()
    start = psi_v[...]
    ag[0, me] = start
    nbr[0, 2] = start
    cur_v[...] = start.astype(F32)
    pl.semaphore_wait(barrier, len(steps) + 2)

    def arrival(p, offset):
        block = ag.at[p, slot(*offset)]
        place = offset[0] * nx + offset[1]
        return remote(block, block, ag_s.at[p], ag_r.at[p, place], device(1, 0))

    def forward(p, parent):
        block = ag.at[p, slot(*parent)]
        for child in kids.get(parent, ()):
            place = child[0] * nx + child[1]
            where = device((child[0] - parent[0]) % nz, (child[1] - parent[1]) % nx)
            remote(block, block, ag_s.at[p], ag_r.at[p, place], where).start()

    def half_blocks(p, offsets):
        stacked = []
        for offset in offsets:
            s = slot(*offset)
            ops = left_v[:, s].reshape(terms * width, width)
            stacked.append((s, jnp.dot(ops, ag[p, s], preferred_element_type=F32)))
        for s, half in stacked:
            for k in range(terms):
                weight = active_ref[0, k, s].astype(F32)
                half_v[k, s] = (half[k * width:(k + 1) * width] * weight).astype(BF16)

    busy = [i for i, offset in enumerate(order) if offset in kids]
    pauses = (4, 8)

    def gather(p, midway=None):
        ready = [(0, 0)]
        for i, offset in enumerate(order):
            arrival(p, offset).wait_recv()
            forward(p, offset)
            ready.append(offset)
            while len(ready) >= 4 and (i >= busy[-1] or i in pauses):
                half_blocks(p, ready[:4])
                ready = ready[4:]
            if midway is not None and i == pauses[-1]:
                midway()
        if ready:
            half_blocks(p, ready)

    def gathered(t):
        halves, rights = [], []
        for k in range(terms):
            s = lax.rem(t + blocks - shift_ref[0, k], blocks)
            halves.append(half_v[k, s])
            rights.append(right_v[k, s])
        return jnp.concatenate(halves, axis=1), jnp.concatenate(rights, axis=1)

    def term_block(t):
        halves, rights = gathered(t)
        return lax.dot_general(halves, rights, (((1,), (1,)), ((), ())), preferred_element_type=F32)

    def scatter_x(q, dz, dx):
        place = dz * others + dx - 1
        return remote(xsend.at[q, place], xrecv.at[q, place], rs_xs.at[q], rs_xr.at[q, dz], device(0, dx))

    def scatter_z(q, dz):
        return remote(zsend.at[q, dz - 1], zrecv.at[q, dz - 1], rs_zs.at[q], rs_zr.at[q], device(dz, 0))

    def scatter_send(q):
        def row(i, carry):
            dz = near_first(nz - 1 - i)
            base = ((z + dz) % nz) * nx
            parts = [term_block(base + (x + dx) % nx) for dx in range(nx)]
            own_acc[dz] = parts[0]
            for dx in x_order:
                xsend[q, dz * others + dx - 1] = parts[dx].astype(BF16)
            for dx in x_order:
                scatter_x(q, dz, dx).start()
            return carry
        lax.fori_loop(0, nz, row, 0)

    def column_sum(q, dz):
        three = pl.ds(dz * others, others)
        remote(xsend.at[q, three], xrecv.at[q, three], rs_xs.at[q], rs_xr.at[q, dz], device(0, 1)).wait_recv()
        total = own_acc[dz]
        for dx in range(1, nx):
            total = total + xrecv[q, dz * others + dx - 1].astype(F32)
        return total

    def encode(ref, block):
        largest = jnp.maximum(jnp.max(jnp.abs(block), keepdims=True), 1e-30)
        exponent = jnp.ceil(jnp.log2(largest)) - 14.0
        ref[:width] = jnp.floor(block * jnp.exp2(-exponent) + 0.5).astype(jnp.int32).astype(jnp.int16)
        ref[width:] = jnp.broadcast_to(exponent, (16, width)).astype(jnp.int32).astype(jnp.int16)

    def decode(ref):
        exponent = ref[width:].astype(jnp.int32).astype(F32)[0:1]
        return ref[:width].astype(jnp.int32).astype(F32) * jnp.exp2(exponent)

    def scatter_finish(q):
        def row(i, carry):
            dz = near_first(nz - 1 - i)
            encode(zsend.at[q, dz - 1], column_sum(q, dz))
            scatter_z(q, dz).start()
            return carry
        lax.fori_loop(0, nz - 1, row, 0)
        total = column_sum(q, 0)
        remote(zsend.at[q], zrecv.at[q], rs_zs.at[q], rs_zr.at[q], device(1, 0)).wait_recv()
        for dz in range(1, nz):
            total = total + decode(zrecv.at[q, dz - 1])
        return total * term_scale

    def scalars_z(q, dz):
        return remote(scz.at[q, z], scz.at[q, z], sc_zs.at[q], sc_zr.at[q], device(dz, 0))

    def scalars_x(q, dx):
        return remote(scx.at[q, x], scx.at[q, x], sc_xs.at[q], sc_xr.at[q], device(0, dx))

    def scalars_start(q, cur, applied):
        rows = lax.broadcasted_iota(jnp.int32, (8, width), 0)
        a = jnp.sum(cur * applied)
        b = jnp.sum(cur * cur)
        c = jnp.sum(applied * applied)
        scz[q, z] = jnp.where(rows == 0, a, jnp.where(rows == 1, b, c))
        for i in range(1, nz):
            scalars_z(q, near_first(nz - i)).start()

    def scalars_middle(q):
        many = scz.at[q, pl.ds(0, nz - 1)]
        remote(many, many, sc_zs.at[q], sc_zr.at[q], device(1, 0)).wait_recv()
        total = scz[q, 0]
        for zz in range(1, nz):
            total = total + scz[q, zz]
        scx[q, x] = total
        for dx in range(1, nx):
            scalars_x(q, dx).start()

    def scalars_end(q):
        many = scx.at[q, pl.ds(0, others)]
        remote(many, many, sc_xs.at[q], sc_xr.at[q], device(0, 1)).wait_recv()
        total = scx[q, 0]
        for xx in range(1, nx):
            total = total + scx[q, xx]
        a, b, c = total[0:1], total[1:2], total[2:3]
        rho = a / b
        norm = b + (STEP * STEP) * jnp.maximum(c - a * rho, 0.0)
        scale = jnp.sqrt(count / norm)
        return scale * (1.0 + STEP * rho), scale * STEP

    def neighbours(n):
        up = remote(nbr.at[n, 2], nbr.at[n, 0], nb_s.at[n, 0], nb_r.at[n, 0], (seg_up, me))
        down = remote(nbr.at[n, 2], nbr.at[n, 1], nb_s.at[n, 1], nb_r.at[n, 1], (seg_down, me))
        return up, down

    has_left = (seg > 0).astype(F32)
    has_right = (seg < nseg - 1).astype(F32)

    def environment(n, cur):
        for copy in neighbours(n):
            copy.wait_recv()
        first = (nbr[n, 0].astype(F32) * has_left).astype(BF16)
        second = (nbr[n, 1].astype(F32) * has_right).astype(BF16)
        both = jnp.concatenate([first, second], axis=0)
        env = lax.dot_general(both, both, (((0,), (0,)), ((), ())), preferred_element_type=F32)
        return jnp.dot(cur, env, precision=lax.Precision.HIGHEST, preferred_element_type=F32) * (0.5 / width)

    forward(0, (0, 0))
    for copy in neighbours(0):
        copy.start()

    for n in range(ITERS):
        if n == 0:
            left_load.wait()
            right_load.wait()
            shift_load.wait()
            active_load.wait()
        gather(n, functools.partial(scalars_middle, n - 1) if n > 0 else None)
        scatter_send(n)
        if n > 0:
            keep, take = scalars_end(n - 1)
            cur = keep * cur_v[...] - take * app_v[...]
            cur_v[...] = cur
            nbr[n, 2] = cur.astype(BF16)
            for copy in neighbours(n):
                copy.start()
            tcur_v[...] = keep * tcur_v[...]
        app_v[...] = environment(n, cur_v[...])
        total = scatter_finish(n)
        if n > 0:
            total = tcur_v[...] - take * total
        applied = total + app_v[...]
        if n < ITERS - 1:
            ag[n + 1, me] = applied.astype(BF16)
            forward(n + 1, (0, 0))
        tcur_v[...] = total
        app_v[...] = applied
        scalars_start(n, cur_v[...], applied)

    scalars_middle(ITERS - 1)
    keep, take = scalars_end(ITERS - 1)
    final = (keep * cur_v[...] - take * app_v[...]).astype(BF16)
    ag[ITERS, me] = final
    forward(ITERS, (0, 0))
    state_store = pltpu.make_async_copy(ag.at[ITERS, me], state_hbm.at[0, 0], load_sem.at[5])
    state_store.start()
    gather(ITERS)

    def values(t, acc):
        halves, rights = gathered(t)
        crossed = jnp.dot(ag[ITERS, t], rights, preferred_element_type=F32)
        crossed = crossed * halves.astype(F32)
        return acc + jnp.sum(crossed.reshape(width // 8, 8, terms * width), axis=0)

    acc = lax.fori_loop(0, blocks, values, jnp.zeros((8, terms * width), F32), unroll=4)
    for k in range(terms):
        rdm_ref[0, k] = jnp.sum(acc[:, k * width:(k + 1) * width]) * (1.0 / count)

    state_store.wait()
    for p in range(ITERS + 1):
        many = ag.at[p, pl.ds(0, nz * nx - 1)]
        remote(many, many, ag_s.at[p], ag_r.at[p, 0], device(1, 0)).wait_send()
    for n in range(ITERS):
        remote(xsend.at[n], xrecv.at[n], rs_xs.at[n], rs_xr.at[n, 0], device(0, 1)).wait_send()
        remote(zsend.at[n], zrecv.at[n], rs_zs.at[n], rs_zr.at[n], device(1, 0)).wait_send()
        many = scz.at[n, pl.ds(0, nz - 1)]
        remote(many, many, sc_zs.at[n], sc_zr.at[n], device(1, 0)).wait_send()
        many = scx.at[n, pl.ds(0, others)]
        remote(many, many, sc_xs.at[n], sc_xr.at[n], device(0, 1)).wait_send()
        for copy in neighbours(n):
            copy.wait_send()


def emit(state_in, pieces_in, state_out, pieces_out, sem):
    copies = [
        pltpu.make_async_copy(state_in, state_out, sem.at[0]),
        pltpu.make_async_copy(pieces_in, pieces_out, sem.at[1]),
    ]
    for copy in copies:
        copy.start()
    for copy in copies:
        copy.wait()


def shards(nseg, nop, psi_start, left_ops, right_ops, shifts, active):
    nx = 4 if nop == 32 else 2
    nz = nop // nx
    terms, blocks, width = left_ops.shape[1], left_ops.shape[2], left_ops.shape[3]
    vmem, dma = pltpu.VMEM, pltpu.SemaphoreType.DMA
    tile = (width, width)
    coded = (width + 16, width)
    state, pieces = pl.pallas_call(
        functools.partial(kernel, nz, nx, nseg, nop),
        out_shape=(
            jax.ShapeDtypeStruct((1, 1) + tile, BF16),
            jax.ShapeDtypeStruct((1, terms), F32),
        ),
        in_specs=[
            pl.BlockSpec(memory_space=pltpu.HBM),
            pl.BlockSpec(memory_space=pltpu.HBM),
            pl.BlockSpec(memory_space=pltpu.HBM),
            pl.BlockSpec(memory_space=pltpu.HBM),
            pl.BlockSpec(memory_space=pltpu.HBM),
        ],
        out_specs=(
            pl.BlockSpec(memory_space=pltpu.HBM),
            pl.BlockSpec(memory_space=pltpu.SMEM),
        ),
        scratch_shapes=[
            vmem(tile, BF16),
            pltpu.SMEM((1, terms), jnp.int32),
            pltpu.SMEM((1, terms, blocks), jnp.int32),
            vmem((terms, blocks) + tile, BF16),
            vmem((terms, blocks) + tile, BF16),
            vmem((terms, blocks) + tile, BF16),
            vmem((ITERS + 1, nop) + tile, BF16),
            vmem((ITERS, nz * (nx - 1)) + tile, BF16),
            vmem((ITERS, nz * (nx - 1)) + tile, BF16),
            vmem((nz,) + tile, F32),
            vmem((ITERS, nz - 1) + coded, jnp.int16),
            vmem((ITERS, nz - 1) + coded, jnp.int16),
            vmem((ITERS, nz, 8, width), F32),
            vmem((ITERS, nx, 8, width), F32),
            vmem((ITERS, 3) + tile, BF16),
            vmem(tile, F32),
            vmem(tile, F32),
            vmem(tile, F32),
            dma((6,)),
            dma((ITERS + 1,)),
            dma((ITERS + 1, nop)),
            dma((ITERS,)),
            dma((ITERS, nz)),
            dma((ITERS,)),
            dma((ITERS,)),
            dma((ITERS,)),
            dma((ITERS,)),
            dma((ITERS,)),
            dma((ITERS,)),
            dma((ITERS, 2)),
            dma((ITERS, 2)),
        ],
        compiler_params=pltpu.CompilerParams(
            collective_id=0, has_side_effects=True, vmem_limit_bytes=63 * 1024 * 1024
        ),
        name="chain",
    )(
        psi_start,
        left_ops.reshape(left_ops.shape[1:]),
        right_ops.reshape(right_ops.shape[1:]),
        shifts,
        active,
    )
    hbm = pl.BlockSpec(memory_space=pltpu.HBM)
    return pl.pallas_call(
        emit,
        out_shape=(
            jax.ShapeDtypeStruct(state.shape, state.dtype),
            jax.ShapeDtypeStruct(pieces.shape, pieces.dtype),
        ),
        in_specs=[hbm, hbm],
        out_specs=(hbm, hbm),
        scratch_shapes=[dma((2,))],
        name="emit",
    )(state, pieces)


def solution(mesh):
    return jax.shard_map(
        functools.partial(shards, mesh.shape["seg"], mesh.shape["op"]),
        mesh=mesh,
        in_specs=(
            P("seg", "op", None, None),
            P("seg", "op", None, None, None),
            P("seg", "op", None, None, None),
            P("seg", "op"),
            P("seg", "op", None),
        ),
        out_specs=(P("seg", "op", None, None), P("seg", "op")),
        check_vma=False,
    )
```

```python
import functools

import jax
import jax.numpy as jnp
from jax import lax
from jax.experimental import pallas as pl
from jax.experimental.pallas import tpu as pltpu
from jax.sharding import PartitionSpec as P

ITERS = 3
STEP = 0.3
MESH = pl.DeviceIdType.MESH
F32 = jnp.float32
BF16 = jnp.bfloat16


TREE = (
    ((1, 0), (0, 0)), ((7, 0), (0, 0)), ((0, 1), (0, 0)), ((0, 3), (0, 0)),
    ((0, 2), (0, 0)), ((2, 0), (0, 0)), ((6, 0), (0, 0)), ((1, 1), (1, 0)),
    ((1, 3), (1, 0)), ((2, 1), (1, 0)), ((1, 2), (0, 2)), ((7, 2), (7, 0)),
    ((2, 3), (2, 0)), ((4, 0), (7, 0)), ((6, 1), (6, 0)), ((6, 3), (6, 0)),
    ((5, 3), (6, 0)), ((3, 2), (0, 2)), ((2, 2), (2, 1)), ((7, 1), (1, 1)),
    ((3, 1), (2, 1)), ((7, 3), (7, 2)), ((4, 3), (4, 0)), ((3, 0), (4, 0)),
    ((3, 3), (2, 3)), ((4, 1), (4, 0)), ((6, 2), (6, 3)), ((5, 1), (6, 1)),
    ((5, 0), (5, 3)), ((4, 2), (3, 2)), ((5, 2), (5, 3)),
)


def gather_tree(nz, nx):
    if (nz, nx) == (8, 4):
        tree = TREE
    else:
        tree = tuple(((dz, 0), (0, 0)) for dz in range(1, nz))
        tree += tuple(((dz, dx), (dz, 0)) for dz in range(nz) for dx in range(1, nx))
    kids = {}
    for child, parent in tree:
        kids.setdefault(parent, []).append(child)

    def hops(child, parent):
        up, right = (child[0] - parent[0]) % nz, (child[1] - parent[1]) % nx
        return min(up, nz - up) + min(right, nx - right)

    for parent, children in kids.items():
        children.sort(key=lambda child: (hops(child, parent), -len(kids.get(child, ()))))
    return [child for child, _ in tree], kids


def kernel(
    nz, nx, nseg, axis_terms,
    psi_hbm, left_hbm, right_hbm, shift_hbm, active_hbm,
    state_hbm, rdm_ref,
    psi_v, shift_ref, active_ref, left_v, right_v, half_v, ag, lsend, lrecv, isend, irecv, own_acc,
    scz, scx, nbr, cur_v, tcur_v, app_v,
    load_sem, ag_s, ag_r, rs_ls, rs_lr, rs_is, rs_ir,
    sc_zs, sc_zr, sc_xs, sc_xr, nb_s, nb_r,
):
    terms, blocks, width = left_v.shape[0], left_v.shape[1], left_v.shape[2]
    count = float(blocks * width * width)
    term_scale = 1.0 / (terms * axis_terms)
    others = nx - 1
    seg = lax.axis_index("seg")
    me = lax.axis_index("op")
    z, x = me // nx, me % nx
    x_order = (1, 3, 2) if nx == 4 else (1,)

    def device(dz, dx):
        return (seg, ((z + dz) % nz) * nx + (x + dx) % nx)

    def slot(dz, dx):
        return ((z + nz - dz) % nz) * nx + (x + nx - dx) % nx

    def remote(src, dst, send_sem, recv_sem, where):
        return pltpu.make_async_remote_copy(
            src_ref=src, dst_ref=dst, send_sem=send_sem, recv_sem=recv_sem,
            device_id=where, device_id_type=MESH,
        )

    def near_first(i):
        hop = (i + 1) // 2
        return (hop + ((i + 1) % 2) * (nz - 2 * hop)) % nz

    psi_load = pltpu.make_async_copy(psi_hbm.at[0, 0], psi_v, load_sem.at[0])
    left_load = pltpu.make_async_copy(left_hbm, left_v, load_sem.at[1])
    right_load = pltpu.make_async_copy(right_hbm, right_v, load_sem.at[2])
    psi_load.start()
    shift_load = pltpu.make_async_copy(shift_hbm, shift_ref, load_sem.at[3])
    active_load = pltpu.make_async_copy(active_hbm, active_ref, load_sem.at[4])
    left_load.start()
    right_load.start()
    shift_load.start()
    active_load.start()

    seg_up = (seg + 1) % nseg
    seg_down = (seg + nseg - 1) % nseg
    order, kids = gather_tree(nz, nx)
    steps = {((c[0] - p[0]) % nz, (c[1] - p[1]) % nx) for p in kids for c in kids[p]}
    steps |= {(dz, 0) for dz in range(1, nz)} | {(0, dx) for dx in range(1, nx)}
    steps |= {((nz - dz) % nz, (nx - dx) % nx) for dz, dx in steps}
    barrier = pltpu.get_barrier_semaphore()
    for dz, dx in sorted(steps):
        pl.semaphore_signal(barrier, inc=1, device_id=device(dz, dx), device_id_type=MESH)
    for other in (seg_up, seg_down):
        pl.semaphore_signal(barrier, inc=1, device_id=(other, me), device_id_type=MESH)
    psi_load.wait()
    start = psi_v[...]
    ag[0, me] = start
    nbr[0, 2] = start
    cur_v[...] = start.astype(F32)
    pl.semaphore_wait(barrier, len(steps) + 2)

    def arrival(p, offset):
        block = ag.at[p, slot(*offset)]
        place = offset[0] * nx + offset[1]
        return remote(block, block, ag_s.at[p], ag_r.at[p, place], device(1, 0))

    def forward(p, parent):
        block = ag.at[p, slot(*parent)]
        for child in kids.get(parent, ()):
            place = child[0] * nx + child[1]
            where = device((child[0] - parent[0]) % nz, (child[1] - parent[1]) % nx)
            remote(block, block, ag_s.at[p], ag_r.at[p, place], where).start()

    def half_blocks(p, offsets):
        stacked = []
        for offset in offsets:
            s = slot(*offset)
            ops = left_v[:, s].reshape(terms * width, width)
            stacked.append((s, jnp.dot(ops, ag[p, s], preferred_element_type=F32)))
        for s, half in stacked:
            for k in range(terms):
                weight = active_ref[0, k, s].astype(F32)
                half_v[k, s] = (half[k * width:(k + 1) * width] * weight).astype(BF16)

    busy = [i for i, offset in enumerate(order) if offset in kids]
    pauses = (4, 8)

    def gather(p, midway=None):
        ready = [(0, 0)]
        for i, offset in enumerate(order):
            arrival(p, offset).wait_recv()
            forward(p, offset)
            ready.append(offset)
            while len(ready) >= 4 and (i >= busy[-1] or i in pauses):
                half_blocks(p, ready[:4])
                ready = ready[4:]
            if midway is not None and i == pauses[-1]:
                midway()
        if ready:
            half_blocks(p, ready)

    def gathered(t):
        halves, rights = [], []
        for k in range(terms):
            s = lax.rem(t + blocks - shift_ref[0, k], blocks)
            halves.append(half_v[k, s])
            rights.append(right_v[k, s])
        return jnp.concatenate(halves, axis=1), jnp.concatenate(rights, axis=1)

    def term_block(t):
        halves, rights = gathered(t)
        return lax.dot_general(halves, rights, (((1,), (1,)), ((), ())), preferred_element_type=F32)

    leaves = [offset for offset in order if offset not in kids]
    inner = [offset for offset in order if offset in kids]
    parent_of = {child: parent for parent in kids for child in kids[parent]}
    place = {offset: i for group in (leaves, inner) for i, offset in enumerate(group)}
    place[(0, 0)] = len(inner)

    def edge(q, offset):
        parent, i = parent_of[offset], place[offset]
        where = device((parent[0] - offset[0]) % nz, (parent[1] - offset[1]) % nx)
        if offset in kids:
            return remote(isend.at[q, i], irecv.at[q, i], rs_is.at[q], rs_ir.at[q, i], where)
        return remote(lsend.at[q, i], lrecv.at[q, i], rs_ls.at[q], rs_lr.at[q, i], where)

    def scatter_send(q):
        todo = leaves[::-1] + inner[::-1] + [(0, 0)]
        for first in range(0, len(todo), 4):
            group = todo[first:first + 4]
            parts = [term_block(slot(*offset)) for offset in group]
            for offset, part in zip(group, parts):
                if offset in kids:
                    own_acc[place[offset]] = part
                else:
                    lsend[q, place[offset]] = part.astype(BF16)
            for offset in group:
                if offset not in kids:
                    edge(q, offset).start()

    def collect(q, offset):
        total = own_acc[place[offset]]
        for child in sorted(kids[offset], key=order.index, reverse=True):
            edge(q, child).wait_recv()
            if child in kids:
                total = total + decode(irecv.at[q, place[child]])
            else:
                total = total + lrecv[q, place[child]].astype(F32)
        return total

    def encode(ref, block):
        largest = jnp.maximum(jnp.max(jnp.abs(block), axis=0, keepdims=True), 1e-30)
        exponent = jnp.ceil(jnp.log2(largest)) - 14.0
        ref[:width] = jnp.floor(block * jnp.exp2(-exponent) + 0.5).astype(jnp.int32).astype(jnp.int16)
        ref[width:] = jnp.broadcast_to(exponent, (16, width)).astype(jnp.int32).astype(jnp.int16)

    def decode(ref):
        exponent = ref[width:].astype(jnp.int32).astype(F32)[0:1]
        return ref[:width].astype(jnp.int32).astype(F32) * jnp.exp2(exponent)

    def scatter_finish(q, midway):
        for i, offset in enumerate(inner[::-1]):
            encode(isend.at[q, place[offset]], collect(q, offset))
            edge(q, offset).start()
            if i == len(inner) // 2:
                midway()
        return collect(q, (0, 0)) * term_scale

    def scalars_z(q, dz):
        return remote(scz.at[q, z], scz.at[q, z], sc_zs.at[q], sc_zr.at[q], device(dz, 0))

    def scalars_x(q, dx):
        return remote(scx.at[q, x], scx.at[q, x], sc_xs.at[q], sc_xr.at[q], device(0, dx))

    def scalars_start(q, cur, applied):
        rows = lax.broadcasted_iota(jnp.int32, (8, width), 0)
        a = jnp.sum(cur * applied)
        b = jnp.sum(cur * cur)
        c = jnp.sum(applied * applied)
        scz[q, z] = jnp.where(rows == 0, a, jnp.where(rows == 1, b, c))
        for i in range(1, nz):
            scalars_z(q, near_first(nz - i)).start()

    def scalars_middle(q):
        many = scz.at[q, pl.ds(0, nz - 1)]
        remote(many, many, sc_zs.at[q], sc_zr.at[q], device(1, 0)).wait_recv()
        total = scz[q, 0]
        for zz in range(1, nz):
            total = total + scz[q, zz]
        scx[q, x] = total
        for dx in range(1, nx):
            scalars_x(q, dx).start()

    def scalars_end(q):
        many = scx.at[q, pl.ds(0, others)]
        remote(many, many, sc_xs.at[q], sc_xr.at[q], device(0, 1)).wait_recv()
        total = scx[q, 0]
        for xx in range(1, nx):
            total = total + scx[q, xx]
        a, b, c = total[0:1], total[1:2], total[2:3]
        rho = a / b
        norm = b + (STEP * STEP) * jnp.maximum(c - a * rho, 0.0)
        scale = jnp.sqrt(count / norm)
        return scale * (1.0 + STEP * rho), scale * STEP

    def neighbours(n):
        up = remote(nbr.at[n, 2], nbr.at[n, 0], nb_s.at[n, 0], nb_r.at[n, 0], (seg_up, me))
        down = remote(nbr.at[n, 2], nbr.at[n, 1], nb_s.at[n, 1], nb_r.at[n, 1], (seg_down, me))
        return up, down

    has_left = (seg > 0).astype(F32)
    has_right = (seg < nseg - 1).astype(F32)

    def environment(n, cur):
        for copy in neighbours(n):
            copy.wait_recv()
        first = (nbr[n, 0].astype(F32) * has_left).astype(BF16)
        second = (nbr[n, 1].astype(F32) * has_right).astype(BF16)
        both = jnp.concatenate([first, second], axis=0)
        env = lax.dot_general(both, both, (((0,), (0,)), ((), ())), preferred_element_type=F32)
        return jnp.dot(cur, env, precision=lax.Precision.HIGHEST, preferred_element_type=F32) * (0.5 / width)

    forward(0, (0, 0))
    for copy in neighbours(0):
        copy.start()

    for n in range(ITERS):
        if n == 0:
            left_load.wait()
            right_load.wait()
            shift_load.wait()
            active_load.wait()
        gather(n, functools.partial(scalars_middle, n - 1) if n > 0 else None)
        scatter_send(n)
        if n > 0:
            keep, take = scalars_end(n - 1)
            cur = keep * cur_v[...] - take * app_v[...]
            cur_v[...] = cur
            nbr[n, 2] = cur.astype(BF16)
            for copy in neighbours(n):
                copy.start()
            tcur_v[...] = keep * tcur_v[...]

        def midway(n=n):
            app_v[...] = environment(n, cur_v[...])

        total = scatter_finish(n, midway)
        if n > 0:
            total = tcur_v[...] - take * total
        applied = total + app_v[...]
        if n < ITERS - 1:
            ag[n + 1, me] = applied.astype(BF16)
            forward(n + 1, (0, 0))
        tcur_v[...] = total
        app_v[...] = applied
        scalars_start(n, cur_v[...], applied)

    scalars_middle(ITERS - 1)
    keep, take = scalars_end(ITERS - 1)
    final = (keep * cur_v[...] - take * app_v[...]).astype(BF16)
    ag[ITERS, me] = final
    forward(ITERS, (0, 0))
    state_store = pltpu.make_async_copy(ag.at[ITERS, me], state_hbm.at[0, 0], load_sem.at[5])
    state_store.start()
    gather(ITERS)

    def values(t, acc):
        halves, rights = gathered(t)
        crossed = jnp.dot(ag[ITERS, t], rights, preferred_element_type=F32)
        crossed = crossed * halves.astype(F32)
        return acc + jnp.sum(crossed.reshape(width // 8, 8, terms * width), axis=0)

    acc = lax.fori_loop(0, blocks, values, jnp.zeros((8, terms * width), F32), unroll=4)
    for k in range(terms):
        rdm_ref[0, k] = jnp.sum(acc[:, k * width:(k + 1) * width]) * (1.0 / count)

    state_store.wait()
    for p in range(ITERS + 1):
        many = ag.at[p, pl.ds(0, nz * nx - 1)]
        remote(many, many, ag_s.at[p], ag_r.at[p, 0], device(1, 0)).wait_send()
    for n in range(ITERS):
        remote(lsend.at[n], lrecv.at[n], rs_ls.at[n], rs_lr.at[n, 0], device(1, 0)).wait_send()
        remote(isend.at[n], irecv.at[n], rs_is.at[n], rs_ir.at[n, 0], device(1, 0)).wait_send()
        many = scz.at[n, pl.ds(0, nz - 1)]
        remote(many, many, sc_zs.at[n], sc_zr.at[n], device(1, 0)).wait_send()
        many = scx.at[n, pl.ds(0, others)]
        remote(many, many, sc_xs.at[n], sc_xr.at[n], device(0, 1)).wait_send()
        for copy in neighbours(n):
            copy.wait_send()


def emit(state_in, pieces_in, state_out, pieces_out, sem):
    copies = [
        pltpu.make_async_copy(state_in, state_out, sem.at[0]),
        pltpu.make_async_copy(pieces_in, pieces_out, sem.at[1]),
    ]
    for copy in copies:
        copy.start()
    for copy in copies:
        copy.wait()


def shards(nseg, nop, psi_start, left_ops, right_ops, shifts, active):
    nx = 4 if nop == 32 else 2
    nz = nop // nx
    terms, blocks, width = left_ops.shape[1], left_ops.shape[2], left_ops.shape[3]
    vmem, dma = pltpu.VMEM, pltpu.SemaphoreType.DMA
    tile = (width, width)
    coded = (width + 16, width)
    order, kids = gather_tree(nz, nx)
    n_inner = len(kids) - 1
    n_leaf = len(order) - n_inner
    state, pieces = pl.pallas_call(
        functools.partial(kernel, nz, nx, nseg, nop),
        out_shape=(
            jax.ShapeDtypeStruct((1, 1) + tile, BF16),
            jax.ShapeDtypeStruct((1, terms), F32),
        ),
        in_specs=[
            pl.BlockSpec(memory_space=pltpu.HBM),
            pl.BlockSpec(memory_space=pltpu.HBM),
            pl.BlockSpec(memory_space=pltpu.HBM),
            pl.BlockSpec(memory_space=pltpu.HBM),
            pl.BlockSpec(memory_space=pltpu.HBM),
        ],
        out_specs=(
            pl.BlockSpec(memory_space=pltpu.HBM),
            pl.BlockSpec(memory_space=pltpu.SMEM),
        ),
        scratch_shapes=[
            vmem(tile, BF16),
            pltpu.SMEM((1, terms), jnp.int32),
            pltpu.SMEM((1, terms, blocks), jnp.int32),
            vmem((terms, blocks) + tile, BF16),
            vmem((terms, blocks) + tile, BF16),
            vmem((terms, blocks) + tile, BF16),
            vmem((ITERS + 1, nop) + tile, BF16),
            vmem((ITERS, n_leaf) + tile, BF16),
            vmem((ITERS, n_leaf) + tile, BF16),
            vmem((ITERS, n_inner) + coded, jnp.int16),
            vmem((ITERS, n_inner) + coded, jnp.int16),
            vmem((n_inner + 1,) + tile, F32),
            vmem((ITERS, nz, 8, width), F32),
            vmem((ITERS, nx, 8, width), F32),
            vmem((ITERS, 3) + tile, BF16),
            vmem(tile, F32),
            vmem(tile, F32),
            vmem(tile, F32),
            dma((6,)),
            dma((ITERS + 1,)),
            dma((ITERS + 1, nop)),
            dma((ITERS,)),
            dma((ITERS, n_leaf)),
            dma((ITERS,)),
            dma((ITERS, n_inner)),
            dma((ITERS,)),
            dma((ITERS,)),
            dma((ITERS,)),
            dma((ITERS,)),
            dma((ITERS, 2)),
            dma((ITERS, 2)),
        ],
        compiler_params=pltpu.CompilerParams(
            collective_id=0, has_side_effects=True, vmem_limit_bytes=63 * 1024 * 1024
        ),
        name="chain",
    )(
        psi_start,
        left_ops.reshape(left_ops.shape[1:]),
        right_ops.reshape(right_ops.shape[1:]),
        shifts,
        active,
    )
    hbm = pl.BlockSpec(memory_space=pltpu.HBM)
    return pl.pallas_call(
        emit,
        out_shape=(
            jax.ShapeDtypeStruct(state.shape, state.dtype),
            jax.ShapeDtypeStruct(pieces.shape, pieces.dtype),
        ),
        in_specs=[hbm, hbm],
        out_specs=(hbm, hbm),
        scratch_shapes=[dma((2,))],
        name="emit",
    )(state, pieces)


def solution(mesh):
    return jax.shard_map(
        functools.partial(shards, mesh.shape["seg"], mesh.shape["op"]),
        mesh=mesh,
        in_specs=(
            P("seg", "op", None, None),
            P("seg", "op", None, None, None),
            P("seg", "op", None, None, None),
            P("seg", "op"),
            P("seg", "op", None),
        ),
        out_specs=(P("seg", "op", None, None), P("seg", "op")),
        check_vma=False,
    )
```

```python
import functools

import jax
import jax.numpy as jnp
from jax import lax
from jax.experimental import pallas as pl
from jax.experimental.pallas import tpu as pltpu
from jax.sharding import PartitionSpec as P

ITERS = 3
STEP = 0.3
MESH = pl.DeviceIdType.MESH
F32 = jnp.float32
BF16 = jnp.bfloat16


TREE = (
    ((1, 0), (0, 0)), ((7, 0), (0, 0)), ((0, 1), (0, 0)), ((0, 3), (0, 0)),
    ((0, 2), (0, 0)), ((2, 0), (0, 0)), ((6, 0), (0, 0)), ((1, 1), (1, 0)),
    ((1, 3), (1, 0)), ((2, 1), (1, 0)), ((1, 2), (0, 2)), ((7, 2), (7, 0)),
    ((2, 3), (2, 0)), ((4, 0), (7, 0)), ((6, 1), (6, 0)), ((6, 3), (6, 0)),
    ((5, 3), (6, 0)), ((3, 2), (0, 2)), ((2, 2), (2, 1)), ((7, 1), (1, 1)),
    ((3, 1), (2, 1)), ((7, 3), (7, 2)), ((4, 3), (4, 0)), ((3, 0), (4, 0)),
    ((3, 3), (2, 3)), ((4, 1), (4, 0)), ((6, 2), (6, 3)), ((5, 1), (6, 1)),
    ((5, 0), (5, 3)), ((4, 2), (3, 2)), ((5, 2), (5, 3)),
)


def gather_tree(nz, nx):
    if (nz, nx) == (8, 4):
        tree = TREE
    else:
        tree = tuple(((dz, 0), (0, 0)) for dz in range(1, nz))
        tree += tuple(((dz, dx), (dz, 0)) for dz in range(nz) for dx in range(1, nx))
    kids = {}
    for child, parent in tree:
        kids.setdefault(parent, []).append(child)

    def hops(child, parent):
        up, right = (child[0] - parent[0]) % nz, (child[1] - parent[1]) % nx
        return min(up, nz - up) + min(right, nx - right)

    for parent, children in kids.items():
        children.sort(key=lambda child: (hops(child, parent), -len(kids.get(child, ()))))
    return [child for child, _ in tree], kids


def kernel(
    nz, nx, nseg, axis_terms,
    psi_hbm, left_hbm, right_hbm, shift_hbm, active_hbm,
    state_hbm, rdm_ref,
    psi_v, shift_ref, active_ref, left_v, right_v, half_v, ag, lsend, lrecv, isend, irecv, own_acc,
    scz, scx, nbr, cur_v, tcur_v, app_v, take_v,
    load_sem, ag_s, ag_r, rs_ls, rs_lr, rs_is, rs_ir,
    sc_zs, sc_zr, sc_xs, sc_xr, nb_s, nb_r,
):
    terms, blocks, width = left_v.shape[0], left_v.shape[1], left_v.shape[2]
    count = float(blocks * width * width)
    term_scale = 1.0 / (terms * axis_terms)
    others = nx - 1
    seg = lax.axis_index("seg")
    me = lax.axis_index("op")
    z, x = me // nx, me % nx
    x_order = (1, 3, 2) if nx == 4 else (1,)

    def device(dz, dx):
        return (seg, ((z + dz) % nz) * nx + (x + dx) % nx)

    def slot(dz, dx):
        return ((z + nz - dz) % nz) * nx + (x + nx - dx) % nx

    def remote(src, dst, send_sem, recv_sem, where):
        return pltpu.make_async_remote_copy(
            src_ref=src, dst_ref=dst, send_sem=send_sem, recv_sem=recv_sem,
            device_id=where, device_id_type=MESH,
        )

    def near_first(i):
        hop = (i + 1) // 2
        return (hop + ((i + 1) % 2) * (nz - 2 * hop)) % nz

    psi_load = pltpu.make_async_copy(psi_hbm.at[0, 0], psi_v, load_sem.at[0])
    left_load = pltpu.make_async_copy(left_hbm, left_v, load_sem.at[1])
    right_load = pltpu.make_async_copy(right_hbm, right_v, load_sem.at[2])
    psi_load.start()
    shift_load = pltpu.make_async_copy(shift_hbm, shift_ref, load_sem.at[3])
    active_load = pltpu.make_async_copy(active_hbm, active_ref, load_sem.at[4])
    left_load.start()
    right_load.start()
    shift_load.start()
    active_load.start()

    seg_up = (seg + 1) % nseg
    seg_down = (seg + nseg - 1) % nseg
    order, kids = gather_tree(nz, nx)
    steps = {((c[0] - p[0]) % nz, (c[1] - p[1]) % nx) for p in kids for c in kids[p]}
    steps |= {(dz, 0) for dz in range(1, nz)} | {(0, dx) for dx in range(1, nx)}
    steps |= {((nz - dz) % nz, (nx - dx) % nx) for dz, dx in steps}
    barrier = pltpu.get_barrier_semaphore()
    for dz, dx in sorted(steps):
        pl.semaphore_signal(barrier, inc=1, device_id=device(dz, dx), device_id_type=MESH)
    for other in (seg_up, seg_down):
        pl.semaphore_signal(barrier, inc=1, device_id=(other, me), device_id_type=MESH)
    psi_load.wait()
    start = psi_v[...]
    ag[0, me] = start
    nbr[0, 2] = start
    cur_v[...] = start.astype(F32)
    pl.semaphore_wait(barrier, len(steps) + 2)

    def arrival(p, offset):
        block = ag.at[p, slot(*offset)]
        place = offset[0] * nx + offset[1]
        return remote(block, block, ag_s.at[p], ag_r.at[p, place], device(1, 0))

    def forward(p, parent):
        block = ag.at[p, slot(*parent)]
        for child in kids.get(parent, ()):
            place = child[0] * nx + child[1]
            where = device((child[0] - parent[0]) % nz, (child[1] - parent[1]) % nx)
            remote(block, block, ag_s.at[p], ag_r.at[p, place], where).start()

    def half_blocks(p, offsets):
        stacked = []
        for offset in offsets:
            s = slot(*offset)
            ops = left_v[:, s].reshape(terms * width, width)
            stacked.append((s, jnp.dot(ops, ag[p, s], preferred_element_type=F32)))
        for s, half in stacked:
            for k in range(terms):
                weight = active_ref[0, k, s].astype(F32)
                half_v[k, s] = (half[k * width:(k + 1) * width] * weight).astype(BF16)

    busy = [i for i, offset in enumerate(order) if offset in kids]
    pauses = (4, 8)

    def gather(p, midway=None):
        ready = [(0, 0)]
        for i, offset in enumerate(order):
            arrival(p, offset).wait_recv()
            forward(p, offset)
            ready.append(offset)
            while len(ready) >= 4 and (i >= busy[-1] or i in pauses):
                half_blocks(p, ready[:4])
                ready = ready[4:]
            if midway is not None and i == pauses[-1]:
                midway()
        if ready:
            half_blocks(p, ready)

    def gathered(t):
        halves, rights = [], []
        for k in range(terms):
            s = lax.rem(t + blocks - shift_ref[0, k], blocks)
            halves.append(half_v[k, s])
            rights.append(right_v[k, s])
        return jnp.concatenate(halves, axis=1), jnp.concatenate(rights, axis=1)

    def term_block(t):
        halves, rights = gathered(t)
        return lax.dot_general(halves, rights, (((1,), (1,)), ((), ())), preferred_element_type=F32)

    leaves = [offset for offset in order if offset not in kids]
    inner = [offset for offset in order if offset in kids]
    parent_of = {child: parent for parent in kids for child in kids[parent]}
    place = {offset: i for group in (leaves, inner) for i, offset in enumerate(group)}
    place[(0, 0)] = len(inner)

    def edge(q, offset):
        parent, i = parent_of[offset], place[offset]
        where = device((parent[0] - offset[0]) % nz, (parent[1] - offset[1]) % nx)
        if offset in kids:
            return remote(isend.at[q, i], irecv.at[q, i], rs_is.at[q], rs_ir.at[q, i], where)
        return remote(lsend.at[q, i], lrecv.at[q, i], rs_ls.at[q], rs_lr.at[q, i], where)

    def scatter_send(q):
        todo = leaves[::-1] + inner[::-1] + [(0, 0)]
        for first in range(0, len(todo), 4):
            group = todo[first:first + 4]
            parts = [term_block(slot(*offset)) for offset in group]
            for offset, part in zip(group, parts):
                if offset in kids:
                    own_acc[place[offset]] = part
                else:
                    lsend[q, place[offset]] = part.astype(BF16)
            for offset in group:
                if offset not in kids:
                    edge(q, offset).start()

    def collect(q, offset):
        total = own_acc[place[offset]]
        for child in sorted(kids[offset], key=order.index, reverse=True):
            edge(q, child).wait_recv()
            if child in kids:
                total = total + decode(irecv.at[q, place[child]])
            else:
                total = total + lrecv[q, place[child]].astype(F32)
        return total

    def encode(ref, block):
        largest = jnp.maximum(jnp.max(jnp.abs(block), axis=0, keepdims=True), 1e-30)
        exponent = jnp.ceil(jnp.log2(largest)) - 14.0
        ref[:width] = jnp.floor(block * jnp.exp2(-exponent) + 0.5).astype(jnp.int32).astype(jnp.int16)
        ref[width:] = jnp.broadcast_to(exponent, (16, width)).astype(jnp.int32).astype(jnp.int16)

    def decode(ref):
        exponent = ref[width:].astype(jnp.int32).astype(F32)[0:1]
        return ref[:width].astype(jnp.int32).astype(F32) * jnp.exp2(exponent)

    def scatter_finish(q, early, late):
        for i, offset in enumerate(inner[::-1]):
            encode(isend.at[q, place[offset]], collect(q, offset))
            edge(q, offset).start()
            if i == len(inner) // 5:
                early()
            if i == (3 * len(inner)) // 4:
                late()
        return collect(q, (0, 0)) * term_scale

    def scalars_z(q, dz):
        return remote(scz.at[q, z], scz.at[q, z], sc_zs.at[q], sc_zr.at[q], device(dz, 0))

    def scalars_x(q, dx):
        return remote(scx.at[q, x], scx.at[q, x], sc_xs.at[q], sc_xr.at[q], device(0, dx))

    def scalars_start(q, cur, applied):
        rows = lax.broadcasted_iota(jnp.int32, (8, width), 0)
        a = jnp.sum(cur * applied, axis=0, keepdims=True)
        b = jnp.sum(cur * cur, axis=0, keepdims=True)
        c = jnp.sum(applied * applied, axis=0, keepdims=True)
        scz[q, z] = jnp.where(rows == 0, a, jnp.where(rows == 1, b, c))
        for i in range(1, nz):
            scalars_z(q, near_first(nz - i)).start()

    def scalars_middle(q):
        many = scz.at[q, pl.ds(0, nz - 1)]
        remote(many, many, sc_zs.at[q], sc_zr.at[q], device(1, 0)).wait_recv()
        total = scz[q, 0]
        for zz in range(1, nz):
            total = total + scz[q, zz]
        scx[q, x] = total
        for dx in range(1, nx):
            scalars_x(q, dx).start()

    def scalars_end(q):
        many = scx.at[q, pl.ds(0, others)]
        remote(many, many, sc_xs.at[q], sc_xr.at[q], device(0, 1)).wait_recv()
        total = scx[q, 0]
        for xx in range(1, nx):
            total = total + scx[q, xx]
        total = jnp.broadcast_to(jnp.sum(total, axis=1, keepdims=True), (8, width))
        a, b, c = total[0:1], total[1:2], total[2:3]
        rho = a / b
        norm = b + (STEP * STEP) * jnp.maximum(c - a * rho, 0.0)
        scale = jnp.sqrt(count / norm)
        return scale * (1.0 + STEP * rho), scale * STEP

    def neighbours(n):
        up = remote(nbr.at[n, 2], nbr.at[n, 0], nb_s.at[n, 0], nb_r.at[n, 0], (seg_up, me))
        down = remote(nbr.at[n, 2], nbr.at[n, 1], nb_s.at[n, 1], nb_r.at[n, 1], (seg_down, me))
        return up, down

    has_left = (seg > 0).astype(F32)
    has_right = (seg < nseg - 1).astype(F32)

    def environment(n, cur):
        for copy in neighbours(n):
            copy.wait_recv()
        first = (nbr[n, 0].astype(F32) * has_left).astype(BF16)
        second = (nbr[n, 1].astype(F32) * has_right).astype(BF16)
        both = jnp.concatenate([first, second], axis=0)
        env = lax.dot_general(both, both, (((0,), (0,)), ((), ())), preferred_element_type=F32)
        return jnp.dot(cur, env, precision=lax.Precision.HIGHEST, preferred_element_type=F32) * (0.5 / width)

    forward(0, (0, 0))
    for copy in neighbours(0):
        copy.start()

    for n in range(ITERS):
        if n == 0:
            left_load.wait()
            right_load.wait()
            shift_load.wait()
            active_load.wait()
        gather(n, functools.partial(scalars_middle, n - 1) if n > 0 else None)
        scatter_send(n)

        def update(n=n):
            if n > 0:
                keep, take = scalars_end(n - 1)
                cur = keep * cur_v[...] - take * app_v[...]
                cur_v[...] = cur
                nbr[n, 2] = cur.astype(BF16)
                for copy in neighbours(n):
                    copy.start()
                tcur_v[...] = keep * tcur_v[...]
                take_v[...] = jnp.broadcast_to(take, take_v.shape)

        def surround(n=n):
            app_v[...] = environment(n, cur_v[...])

        total = scatter_finish(n, update, surround)
        if n > 0:
            total = tcur_v[...] - take_v[0:1] * total
        applied = total + app_v[...]
        if n < ITERS - 1:
            ag[n + 1, me] = applied.astype(BF16)
            forward(n + 1, (0, 0))
        tcur_v[...] = total
        app_v[...] = applied
        scalars_start(n, cur_v[...], applied)

    scalars_middle(ITERS - 1)
    keep, take = scalars_end(ITERS - 1)
    final = (keep * cur_v[...] - take * app_v[...]).astype(BF16)
    ag[ITERS, me] = final
    forward(ITERS, (0, 0))
    state_store = pltpu.make_async_copy(ag.at[ITERS, me], state_hbm.at[0, 0], load_sem.at[5])
    state_store.start()
    gather(ITERS)

    def values(t, acc):
        halves, rights = gathered(t)
        crossed = jnp.dot(ag[ITERS, t], rights, preferred_element_type=F32)
        crossed = crossed * halves.astype(F32)
        return acc + jnp.sum(crossed.reshape(width // 8, 8, terms * width), axis=0)

    acc = lax.fori_loop(0, blocks, values, jnp.zeros((8, terms * width), F32), unroll=4)
    for k in range(terms):
        rdm_ref[0, k] = jnp.sum(acc[:, k * width:(k + 1) * width]) * (1.0 / count)

    state_store.wait()
    for p in range(ITERS + 1):
        many = ag.at[p, pl.ds(0, nz * nx - 1)]
        remote(many, many, ag_s.at[p], ag_r.at[p, 0], device(1, 0)).wait_send()
    for n in range(ITERS):
        remote(lsend.at[n], lrecv.at[n], rs_ls.at[n], rs_lr.at[n, 0], device(1, 0)).wait_send()
        remote(isend.at[n], irecv.at[n], rs_is.at[n], rs_ir.at[n, 0], device(1, 0)).wait_send()
        many = scz.at[n, pl.ds(0, nz - 1)]
        remote(many, many, sc_zs.at[n], sc_zr.at[n], device(1, 0)).wait_send()
        many = scx.at[n, pl.ds(0, others)]
        remote(many, many, sc_xs.at[n], sc_xr.at[n], device(0, 1)).wait_send()
        for copy in neighbours(n):
            copy.wait_send()


def emit(state_in, pieces_in, state_out, pieces_out, sem):
    copies = [
        pltpu.make_async_copy(state_in, state_out, sem.at[0]),
        pltpu.make_async_copy(pieces_in, pieces_out, sem.at[1]),
    ]
    for copy in copies:
        copy.start()
    for copy in copies:
        copy.wait()


def shards(nseg, nop, psi_start, left_ops, right_ops, shifts, active):
    nx = 4 if nop == 32 else 2
    nz = nop // nx
    terms, blocks, width = left_ops.shape[1], left_ops.shape[2], left_ops.shape[3]
    vmem, dma = pltpu.VMEM, pltpu.SemaphoreType.DMA
    tile = (width, width)
    coded = (width + 16, width)
    order, kids = gather_tree(nz, nx)
    n_inner = len(kids) - 1
    n_leaf = len(order) - n_inner
    state, pieces = pl.pallas_call(
        functools.partial(kernel, nz, nx, nseg, nop),
        out_shape=(
            jax.ShapeDtypeStruct((1, 1) + tile, BF16),
            jax.ShapeDtypeStruct((1, terms), F32),
        ),
        in_specs=[
            pl.BlockSpec(memory_space=pltpu.HBM),
            pl.BlockSpec(memory_space=pltpu.HBM),
            pl.BlockSpec(memory_space=pltpu.HBM),
            pl.BlockSpec(memory_space=pltpu.HBM),
            pl.BlockSpec(memory_space=pltpu.HBM),
        ],
        out_specs=(
            pl.BlockSpec(memory_space=pltpu.HBM),
            pl.BlockSpec(memory_space=pltpu.SMEM),
        ),
        scratch_shapes=[
            vmem(tile, BF16),
            pltpu.SMEM((1, terms), jnp.int32),
            pltpu.SMEM((1, terms, blocks), jnp.int32),
            vmem((terms, blocks) + tile, BF16),
            vmem((terms, blocks) + tile, BF16),
            vmem((terms, blocks) + tile, BF16),
            vmem((ITERS + 1, nop) + tile, BF16),
            vmem((ITERS, n_leaf) + tile, BF16),
            vmem((ITERS, n_leaf) + tile, BF16),
            vmem((ITERS, n_inner) + coded, jnp.int16),
            vmem((ITERS, n_inner) + coded, jnp.int16),
            vmem((n_inner + 1,) + tile, F32),
            vmem((ITERS, nz, 8, width), F32),
            vmem((ITERS, nx, 8, width), F32),
            vmem((ITERS, 3) + tile, BF16),
            vmem(tile, F32),
            vmem(tile, F32),
            vmem(tile, F32),
            vmem((8, width), F32),
            dma((6,)),
            dma((ITERS + 1,)),
            dma((ITERS + 1, nop)),
            dma((ITERS,)),
            dma((ITERS, n_leaf)),
            dma((ITERS,)),
            dma((ITERS, n_inner)),
            dma((ITERS,)),
            dma((ITERS,)),
            dma((ITERS,)),
            dma((ITERS,)),
            dma((ITERS, 2)),
            dma((ITERS, 2)),
        ],
        compiler_params=pltpu.CompilerParams(
            collective_id=0, has_side_effects=True, vmem_limit_bytes=63 * 1024 * 1024
        ),
        name="chain",
    )(
        psi_start,
        left_ops.reshape(left_ops.shape[1:]),
        right_ops.reshape(right_ops.shape[1:]),
        shifts,
        active,
    )
    hbm = pl.BlockSpec(memory_space=pltpu.HBM)
    return pl.pallas_call(
        emit,
        out_shape=(
            jax.ShapeDtypeStruct(state.shape, state.dtype),
            jax.ShapeDtypeStruct(pieces.shape, pieces.dtype),
        ),
        in_specs=[hbm, hbm],
        out_specs=(hbm, hbm),
        scratch_shapes=[dma((2,))],
        name="emit",
    )(state, pieces)


def solution(mesh):
    return jax.shard_map(
        functools.partial(shards, mesh.shape["seg"], mesh.shape["op"]),
        mesh=mesh,
        in_specs=(
            P("seg", "op", None, None),
            P("seg", "op", None, None, None),
            P("seg", "op", None, None, None),
            P("seg", "op"),
            P("seg", "op", None),
        ),
        out_specs=(P("seg", "op", None, None), P("seg", "op")),
        check_vma=False,
    )
```
